512 devices in a mesh: req: 32 (over x, y, core), ctx: 16 (over z).
Axes of the slice: x: 4, y: 4, z: 16, core: 2. Of those that a mesh axis runs over, the one named last changes fastest.
Arguments:
- keys: bfloat16 [131072, 1024], P(('req', 'ctx')), parts along dimension 0, may hold values from -8 to 8
- values: bfloat16 [131072, 1024], P(('req', 'ctx')), parts along dimension 0, may hold values from -6 to 6
- obs_queries: bfloat16 [12288, 8192], P(('req', 'ctx')), parts along dimension 0, may hold values from -120 to 120
- dec_queries: bfloat16 [2048, 1, 8192], P(('req', 'ctx')), parts along dimension 0, may hold values from -120 to 120
- kept_blocks: int32 [256, 32], P('req'), parts along dimension 0, may hold values from -1 to 31, as said below
- kept_counts: int32 [256], P('req'), parts along dimension 0, may hold values from 8 to 32
- dec_lengths: int32 [2048], P('req'), parts along dimension 0, may hold values from 128 to 4096
- out_proj: bfloat16 [8192, 4096], P('ctx'), may hold values from -0.5 to 0.5
Outputs:
- pooled: float32 [8, 131072], P(None, ('req', 'ctx')), parts along dimension 1
- decoded: bfloat16 [2048, 1, 4096], P(('req', 'ctx')), parts along dimension 0
The draws below stay inside these ranges and needn't reach their ends.
There are 32 independent parts, one for each index of `req`. The reference program is written for one: setup_inputs(seed, part) draws one part's arguments, and reference() takes and returns one part's arrays. A program takes and returns all parts, laid end to end along the dimension named above; an argument that names none is the same for every part. Nothing has to cross between parts.
Inputs may be any that keep to these rules, and one draw needn't show every extreme that they name: For each KV head g the first kept_counts[g] entries of kept_blocks[g] are distinct block numbers that always include 0 and 31; the later entries are -1.
All inputs are finite; a program needn't handle non-finite values.
Results may differ from the reference program's by a relative error of at most 0.018.
Values may be sent and summed in bfloat16 or wider, within the bound.
No kernel may reach another device: no remote copies, remote signals or barrier semaphores. Data moves between devices by JAX's collectives and lax.ppermute only.
A program may use at most 128 MiB of HBM per device.

```python
import jax
import jax.numpy as jnp
from jax import lax

H = 64
KVH = 8
HD = 128
GROUP = 8
SEQ = 4096
BLOCK = 128
NB = 32
OBS = 384
POOL = 7
ROWS = 64
STEPS = 1
DOUT = 4096


def random_fields(base_key):
    key_keys, key_window, key_decode = jax.random.split(base_key, 3)
    key_field = jax.random.normal(key_keys, (SEQ, KVH, HD), jnp.float32)
    window = jax.random.normal(key_window, (OBS, KVH, GROUP, HD), jnp.float32)
    decode = jax.random.normal(key_decode, (ROWS, STEPS, KVH, GROUP, HD), jnp.float32)
    key_field = jnp.clip(key_field, -8.0, 8.0)
    window = jnp.clip(window, -120.0, 120.0)
    decode = jnp.clip(decode, -120.0, 120.0)
    return (key_field.reshape(SEQ, KVH * HD), window.reshape(OBS, H * HD), decode.reshape(ROWS, STEPS, H * HD))


def draw_keys(key, part):
    return random_fields(jax.random.fold_in(key, 7))[0].astype(jnp.bfloat16)


def draw_obs_queries(key, part):
    return random_fields(jax.random.fold_in(key, 7))[1].astype(jnp.bfloat16)


def draw_dec_queries(key, part):
    return random_fields(jax.random.fold_in(key, 7))[2].astype(jnp.bfloat16)


def kept_lists(base_key):
    key_count, key_order, key_middle = jax.random.split(base_key, 3)
    fewest = max(2, NB // 4)
    counts = jax.random.randint(key_count, (KVH,), fewest, NB + 1, jnp.int32)
    ordering = jax.random.permutation(key_order, KVH)
    counts = counts.at[ordering[0]].set(NB).at[ordering[1]].set(fewest)
    middle = jax.vmap(lambda single: jax.random.permutation(single, NB - 2))(jax.random.split(key_middle, KVH)) + 1
    end_blocks = jnp.broadcast_to(jnp.array([0, NB - 1], jnp.int32), (KVH, 2))
    complete = jnp.concatenate([end_blocks, middle.astype(jnp.int32)], axis=1)
    slot_index = jnp.arange(NB, dtype=jnp.int32)[None, :]
    blocks = jnp.where(slot_index < counts[:, None], complete, -1)
    return (blocks.astype(jnp.int32), counts.astype(jnp.int32))


def draw_kept_blocks(key, part):
    return kept_lists(jax.random.fold_in(key, 3))[0]


def draw_kept_counts(key, part):
    return kept_lists(jax.random.fold_in(key, 3))[1]


def draw_dec_lengths(key, part):
    lengths = jax.random.randint(jax.random.fold_in(key, 1), (ROWS,), BLOCK, SEQ + 1, jnp.int32)
    ordering = jax.random.permutation(jax.random.fold_in(key, 2), ROWS)
    return lengths.at[ordering[0]].set(SEQ).at[ordering[1]].set(BLOCK).astype(jnp.int32)


def level_of(rng, dims, cuts, least, high):
    factor_of = 1.0
    for axis_at, blocks in cuts:
        draws = jax.random.uniform(jax.random.fold_in(jax.random.fold_in(rng, 6), axis_at), (blocks,), jnp.float32, least / len(cuts), high / len(cuts))
        factor_of = factor_of * jnp.repeat(jnp.exp(draws), dims[axis_at] // blocks).reshape((-1,) + (1,) * (len(dims) - 1 - axis_at))
    return factor_of


def centred(rng, shape, scale, bound, pieces=(), kind=jnp.bfloat16):
    result = jax.random.normal(rng, shape, jnp.float32) * scale
    if len(pieces) > 0:
        result = level_of(rng, shape, pieces, -0.22, 0.18) * result
    return jnp.clip(result, min=-bound, max=bound).astype(kind)


def setup_inputs(seed: int = 0, part: int = 0) -> dict:
    splits = jax.random.split(jax.random.key(seed), 9)
    part_splits = jax.random.split(jax.random.fold_in(splits[8], part), 9)
    keys = draw_keys(jax.random.fold_in(jax.random.fold_in(splits[8], part), 71), part)
    values = centred(part_splits[1], (SEQ, KVH * HD), 1.0, 6.0, ((0, 16),))
    obs_queries = draw_obs_queries(jax.random.fold_in(jax.random.fold_in(splits[8], part), 71), part)
    dec_queries = draw_dec_queries(jax.random.fold_in(jax.random.fold_in(splits[8], part), 71), part)
    kept_blocks = draw_kept_blocks(jax.random.fold_in(jax.random.fold_in(splits[8], part), 71), part)
    kept_counts = draw_kept_counts(jax.random.fold_in(jax.random.fold_in(splits[8], part), 71), part)
    dec_lengths = draw_dec_lengths(jax.random.fold_in(jax.random.fold_in(splits[8], part), 71), part)
    out_proj = centred(splits[7], (H * HD, DOUT), HD ** -0.5, 0.5, ((0, 16),))
    return dict(keys=keys, values=values, obs_queries=obs_queries, dec_queries=dec_queries, kept_blocks=kept_blocks, kept_counts=kept_counts, dec_lengths=dec_lengths, out_proj=out_proj)


def window_columns(operands):
    query_group, key_group = operands
    scores = jnp.dot(query_group, key_group.T, preferred_element_type=jnp.float32) * (HD ** -0.5)
    scores = scores.reshape(GROUP, OBS, SEQ)
    query_place = SEQ - OBS + jnp.arange(OBS, dtype=jnp.int32)
    visible = query_place[:, None] >= jnp.arange(SEQ, dtype=jnp.int32)[None, :]
    scores = jnp.where(visible[None], scores, -1e30)
    row_max = jnp.max(scores, axis=2, keepdims=True)
    weights = jnp.where(visible[None], jnp.exp(scores - row_max), 0.0)
    probability = weights / jnp.sum(weights, axis=2, keepdims=True)
    return jnp.sum(probability, axis=(0, 1))


def decode_head(operands, row_lengths):
    query_head, key_all, value_all, places, usable = operands
    key_pick = key_all[places]
    value_pick = value_all[places]
    scores = jnp.einsum("rgd,kd->grk", query_head.astype(jnp.float32), key_pick.astype(jnp.float32)) * (HD ** -0.5)
    seen = usable[None, :] & (places[None, :] < row_lengths[:, None])
    scores = jnp.where(seen[None], scores, -1e30)
    row_max = jnp.max(scores, axis=2, keepdims=True)
    weights = jnp.where(seen[None], jnp.exp(scores - row_max), 0.0)
    total = jnp.sum(weights, axis=2, keepdims=True)
    rounded = weights.astype(jnp.bfloat16)
    summed = jnp.einsum("grk,kd->grd", rounded.astype(jnp.float32), value_pick.astype(jnp.float32))
    return (summed / total).astype(jnp.bfloat16)


def reference(keys, values, obs_queries, dec_queries, kept_blocks, kept_counts, dec_lengths, out_proj):
    key_heads = keys.reshape(SEQ, KVH, HD).transpose(1, 0, 2)
    value_heads = values.reshape(SEQ, KVH, HD).transpose(1, 0, 2)
    window = obs_queries.reshape(OBS, KVH, GROUP, HD).transpose(1, 2, 0, 3).reshape(KVH, GROUP * OBS, HD)
    column = lax.map(window_columns, (window, key_heads))
    half_width = (POOL - 1) // 2
    padded = jnp.pad(column, ((0, 0), (half_width, half_width)))
    pooled = padded[:, 0:SEQ]
    for offset in range(1, POOL):
        pooled = pooled + padded[:, offset:offset + SEQ]
    pooled = pooled / POOL
    slot_valid = jnp.arange(NB, dtype=jnp.int32)[None, :] < kept_counts[:, None]
    places = (jnp.maximum(kept_blocks, 0)[:, :, None] * BLOCK + jnp.arange(BLOCK, dtype=jnp.int32)[None, None, :])
    places = places.reshape(KVH, NB * BLOCK).astype(jnp.int32)
    usable = jnp.broadcast_to(slot_valid[:, :, None], (KVH, NB, BLOCK)).reshape(KVH, NB * BLOCK)
    row_lengths = jnp.repeat(dec_lengths, STEPS)
    decode_rows = dec_queries.reshape(ROWS * STEPS, KVH, GROUP, HD).transpose(1, 0, 2, 3)
    attended = lax.map(lambda operands: decode_head(operands, row_lengths), (decode_rows, key_heads, value_heads, places, usable))
    flattened = attended.transpose(2, 0, 1, 3).reshape(ROWS * STEPS, H * HD)
    decoded = jnp.dot(flattened, out_proj, preferred_element_type=jnp.float32).astype(jnp.bfloat16)
    return pooled, decoded.reshape(ROWS, STEPS, DOUT)
```

```python
import functools

import jax
import jax.numpy as jnp
from jax import lax
from jax.experimental import pallas as pl
from jax.experimental.pallas import tpu as pltpu
from jax.sharding import PartitionSpec as P

H = 64
KVH = 8
HD = 128
GROUP = 8
BLOCK = 128
NB = 32
SEQ = 4096
OBS = 384
POOL = 7
ROWS = 64
DOUT = 4096
N = 16
OBS_L = OBS // N
ROW_L = ROWS // N
HQ = 4
K0 = 0
V0 = 128
Q0 = 256
D0 = Q0 + HQ * OBS_L
CH = D0 + GROUP * ROW_L
EXTRA = 128
FOLD = HD ** (-0.5) * 1.4426950408889634
NEG = -1e30
FAR = 1 << 30
BF = jnp.bfloat16
F32 = jnp.float32
VMEM = pl.BlockSpec(memory_space=pltpu.VMEM)
SMEM = pl.BlockSpec(memory_space=pltpu.SMEM)


def params():
    return pltpu.CompilerParams(vmem_limit_bytes=60 << 20)


def pack_kernel(k_ref, v_ref, q_ref, d_ref, out_ref):
    for dest in range(N):
        head, half = dest // 2, dest % 2
        rows = slice(half * BLOCK, (half + 1) * BLOCK)
        cols = slice(head * HD, (head + 1) * HD)
        out_ref[dest, K0 : K0 + BLOCK, :] = k_ref[rows, cols]
        out_ref[dest, V0 : V0 + BLOCK, :] = v_ref[rows, cols]
        pieces = []
        for h in range(HQ):
            at = (dest * HQ + h) * HD
            pieces.append(q_ref[:, at : at + HD].astype(F32))
        out_ref[dest, Q0:D0, :] = jnp.concatenate(pieces, axis=0).astype(BF)
        pieces = []
        for h in range(GROUP):
            at = (head * GROUP + h) * HD
            pieces.append(d_ref[:, at : at + HD].astype(F32))
        out_ref[dest, D0:CH, :] = jnp.concatenate(pieces, axis=0).astype(BF)


def pack(keys, values, obs, dec):
    return pl.pallas_call(
        pack_kernel,
        out_shape=jax.ShapeDtypeStruct((N, CH, HD), BF),
        in_specs=[VMEM] * 4,
        out_specs=VMEM,
        compiler_params=params(),
        name="pack",
    )(keys, values, obs, dec)


def dot_t(a, b):
    return lax.dot_general(a, b, (((1,), (1,)), ((), ())), preferred_element_type=F32)


DROWS = 128


def decode_kernel(c_ref, r_ref, kept_ref, len_ref, send_ref, keep_ref, stat_ref):
    half = c_ref[0]
    key = r_ref[:, K0 : K0 + BLOCK, :].reshape(N * BLOCK, HD)
    val = r_ref[:, V0 : V0 + BLOCK, :].reshape(N * BLOCK, HD)
    lane = lax.broadcasted_iota(jnp.int32, (DROWS // 2, HD), 1)
    per = DROWS // (GROUP * ROW_L)
    for chunk in range(ROWS * GROUP // DROWS):
        query = r_ref[chunk * per : (chunk + 1) * per, D0:CH, :].reshape(DROWS, HD)
        scores = dot_t(query, key)
        seen = kept_ref[...] < len_ref[chunk * DROWS : (chunk + 1) * DROWS, :]
        scores = jnp.where(seen, scores, NEG)
        top = jnp.max(scores, axis=1, keepdims=True).astype(BF).astype(F32)
        weights = jnp.where(seen, jnp.exp2((scores - top) * FOLD), 0.0)
        total = jnp.sum(weights, axis=1, keepdims=True)
        summed = jnp.dot(weights.astype(BF), val, preferred_element_type=F32)

        def halves(x):
            x = x.reshape(per, 2, HQ * ROW_L, x.shape[1])
            low = x[:, 0].reshape(DROWS // 2, x.shape[3])
            high = x[:, 1].reshape(DROWS // 2, x.shape[3])
            mine = jnp.where(half == 0, low, high)
            other = jnp.where(half == 0, high, low)
            return mine, other

        top_mine, top_other = halves(jnp.broadcast_to(top, (DROWS, HD)))
        total_mine, total_other = halves(jnp.broadcast_to(total, (DROWS, HD)))
        sum_mine, sum_other = halves(summed)
        coarse = total_other.astype(BF).astype(F32)
        stat = jnp.where(
            lane == 0, top_other, jnp.where(lane == 1, coarse, total_other - coarse)
        )
        at = slice(chunk * DROWS // 2, (chunk + 1) * DROWS // 2)
        send_ref[at, 0:HD] = sum_other.astype(BF)
        send_ref[at, HD : 2 * HD] = stat.astype(BF)
        keep_ref[at, :] = sum_mine
        stat_ref[at, :] = jnp.where(lane == 0, top_mine, total_mine)


def decode(half, received, kept, lens):
    rows = ROWS * HQ
    return pl.pallas_call(
        decode_kernel,
        out_shape=(
            jax.ShapeDtypeStruct((rows, 2 * HD), BF),
            jax.ShapeDtypeStruct((rows, HD), F32),
            jax.ShapeDtypeStruct((rows, HD), F32),
        ),
        in_specs=[SMEM, VMEM, VMEM, VMEM],
        out_specs=(VMEM, VMEM, VMEM),
        compiler_params=params(),
        name="decode",
    )(half, received, kept, lens)


def project_kernel(other_ref, keep_ref, stat_ref, w_ref, out_ref):
    rows = ROWS * HQ
    other = other_ref[...].astype(F32)
    top_o = other[:, HD : HD + 1]
    total_o = other[:, HD + 1 : HD + 2] + other[:, HD + 2 : HD + 3]
    top_m = stat_ref[:, 0:1]
    total_m = stat_ref[:, 1:2]
    top = jnp.maximum(top_o, top_m)
    fac_o = jnp.exp2((top_o - top) * FOLD)
    fac_m = jnp.exp2((top_m - top) * FOLD)
    total = total_o * fac_o + total_m * fac_m
    mixed = other[:, 0:HD] * fac_o + keep_ref[...] * fac_m
    attended = (mixed / total).astype(BF)
    out_row = lax.broadcasted_iota(jnp.int32, (ROWS, rows), 0)
    in_row = lax.broadcasted_iota(jnp.int32, (ROWS, rows), 1)
    base = (out_row >> 2) * (HQ * ROW_L) + (out_row & 3)
    parts = []
    for h in range(HQ):
        pick = jnp.where(in_row == base + h * ROW_L, 1.0, 0.0).astype(BF)
        parts.append(jnp.dot(pick, attended, preferred_element_type=F32).astype(BF))
    flat = jnp.concatenate(parts, axis=1)
    step = 512
    for col in range(0, DOUT, step):
        product = jnp.dot(flat, w_ref[:, col : col + step], preferred_element_type=F32)
        for dest in range(N):
            out_ref[dest, :, col : col + step] = product[
                dest * ROW_L : (dest + 1) * ROW_L, :
            ].astype(BF)


def project(other, keep, stat, w):
    return pl.pallas_call(
        project_kernel,
        out_shape=jax.ShapeDtypeStruct((N, ROW_L, DOUT), BF),
        in_specs=[VMEM] * 4,
        out_specs=VMEM,
        compiler_params=params(),
        name="project",
    )(other, keep, stat, w)


WSRC = 4
WROWS = WSRC * HQ * OBS_L


def window_kernel(c_ref, r_ref, x_ref, out_ref, s_ref, acc_ref):
    half = c_ref[0]
    acc_ref[...] = jnp.zeros_like(acc_ref)
    row = lax.broadcasted_iota(jnp.int32, (WROWS, BLOCK), 0)
    lane = lax.broadcasted_iota(jnp.int32, (WROWS, BLOCK), 1)
    local = (row // (HQ * OBS_L)) * OBS_L + row % OBS_L
    diff = lane - local
    for chunk in range(N // WSRC):
        query = r_ref[chunk * WSRC : (chunk + 1) * WSRC, Q0:D0, :].reshape(WROWS, HD)
        place = SEQ - OBS + chunk * WSRC * OBS_L
        peak = None
        for side in range(2):
            parity = half if side == 0 else 1 - half
            for pair in range(N // 2):
                if side == 0:
                    key = r_ref[2 * pair : 2 * pair + 2, K0 : K0 + BLOCK, :]
                else:
                    key = x_ref[2 * pair : 2 * pair + 2]
                scores = dot_t(query, key.reshape(2 * BLOCK, HD))
                if pair == N // 2 - 1:
                    shown = []
                    for j in range(2):
                        start = (2 * (2 * pair + j) + parity) * BLOCK
                        part = scores[:, j * BLOCK : (j + 1) * BLOCK]
                        shown.append(jnp.where(diff <= place - start, part, NEG))
                    scores = jnp.concatenate(shown, axis=1)
                at = (side * (N // 2) + pair) * 2 * BLOCK
                s_ref[:, at : at + 2 * BLOCK] = scores
                best = jnp.maximum(scores[:, 0:BLOCK], scores[:, BLOCK:])
                peak = best if peak is None else jnp.maximum(peak, best)
        top = jnp.max(peak, axis=1, keepdims=True) * FOLD
        total = jnp.zeros((WROWS, BLOCK), F32)
        for b in range(NB):
            at = slice(b * BLOCK, (b + 1) * BLOCK)
            weight = jnp.exp2(s_ref[:, at] * FOLD - top)
            s_ref[:, at] = weight
            total = total + weight
        share = 1.0 / jnp.sum(total, axis=1, keepdims=True)
        share = jnp.broadcast_to(share, (WROWS, BLOCK))
        for b in range(NB):
            at = slice(b * BLOCK, (b + 1) * BLOCK)
            part = s_ref[:, at] * share
            acc_ref[b] += jnp.sum(part.reshape(WROWS // 8, 8, BLOCK), axis=0)
    sums = jnp.sum(acc_ref[...], axis=1)
    mine, other = sums[0:N], sums[N:NB]
    out_ref[0] = jnp.where(half == 0, mine, other)
    out_ref[1] = jnp.where(half == 0, other, mine)


def window(half, received, partner):
    return pl.pallas_call(
        window_kernel,
        out_shape=jax.ShapeDtypeStruct((2, N, BLOCK), F32),
        in_specs=[SMEM, VMEM, VMEM],
        out_specs=VMEM,
        scratch_shapes=[
            pltpu.VMEM((WROWS, SEQ), F32),
            pltpu.VMEM((NB, 8, BLOCK), F32),
        ],
        compiler_params=params(),
        name="window",
    )(half, received, partner)


def shards(keys, values, obs_queries, dec_queries, kept_blocks, kept_counts, dec_lengths, out_proj):
    me = lax.axis_index("ctx")
    half = lax.rem(me, 2)
    head = me // 2
    swap = [(i, i ^ 1) for i in range(N)]
    half_arg = half[None].astype(jnp.int32)

    sent = pack(keys, values, obs_queries, dec_queries.reshape(ROW_L, H * HD))
    received = lax.all_to_all(sent, "ctx", 0, 0, tiled=True)
    partner = lax.ppermute(received[:, K0 : K0 + BLOCK, :], "ctx", swap)

    blocks = lax.dynamic_slice_in_dim(kept_blocks, head, 1, 0)
    count = lax.dynamic_slice_in_dim(kept_counts, head, 1, 0)
    mine = 2 * jnp.arange(N, dtype=jnp.int32) + half
    named = (blocks == mine[:, None]) & (jnp.arange(NB, dtype=jnp.int32)[None, :] < count)
    hit = jnp.any(named, axis=1)
    places = mine[:, None] * BLOCK + jnp.arange(BLOCK, dtype=jnp.int32)[None, :]
    kept = jnp.where(hit[:, None], places, FAR).reshape(1, N * BLOCK)
    lens = jnp.broadcast_to(dec_lengths.reshape(N, 1, ROW_L), (N, GROUP, ROW_L))
    lens = lens.reshape(N * GROUP * ROW_L, 1)

    send, keep, stat = decode(half_arg, received, kept, lens)
    other = lax.ppermute(send, "ctx", swap)
    product = project(other, keep, stat, out_proj)

    sums = window(half_arg, received, partner)
    low, high = sums[0], sums[1]
    reach = (POOL - 1) // 2
    edge = jnp.zeros((1, reach), F32)
    left = jnp.concatenate([edge, high[:-1, BLOCK - reach :]], axis=0)
    right = jnp.concatenate([low[1:, :reach], edge], axis=0)
    halo = jnp.concatenate([left, right, jnp.zeros((N, BLOCK - 2 * reach), F32)], axis=1)
    cols = jnp.stack([low, high, halo, jnp.zeros_like(low)], axis=1).astype(BF)
    both = jnp.concatenate([product, cols], axis=2)
    back = lax.all_to_all(both, "ctx", 0, 0, tiled=True)
    decoded = jnp.sum(back[:, :, :DOUT].astype(F32), axis=0).astype(BF)
    column = back[:, :, DOUT:].astype(F32).reshape(KVH, 2, ROW_L, BLOCK).sum(axis=1)
    padded = jnp.concatenate(
        [column[:, 2, :reach], column[:, 0], column[:, 1], column[:, 2, reach : 2 * reach]], axis=1
    )
    width = 2 * BLOCK
    pooled = padded[:, 0:width]
    for offset in range(1, POOL):
        pooled = pooled + padded[:, offset : offset + width]
    pooled = pooled / POOL
    return pooled, decoded[:, None, :]


def solution(mesh):
    return jax.shard_map(
        shards,
        mesh=mesh,
        in_specs=(
            P(("req", "ctx"), None),
            P(("req", "ctx"), None),
            P(("req", "ctx"), None),
            P(("req", "ctx"), None, None),
            P("req", None),
            P("req"),
            P("req"),
            P("ctx", None),
        ),
        out_specs=(P(None, ("req", "ctx")), P(("req", "ctx"), None, None)),
        check_vma=False,
    )
```

```python
import jax
import jax.numpy as jnp
from jax import lax
from jax.experimental import pallas as pl
from jax.experimental.pallas import tpu as pltpu
from jax.sharding import PartitionSpec as P


H = 64
KVH = 8
HD = 128
GROUP = 8
BLOCK = 128
NB = 32
SEQ = 4096
OBS = 384
POOL = 7
ROWS = 64
DOUT = 4096
N = 16
OBS_L = OBS // N
ROW_L = ROWS // N
HQ = 4
K0 = 0
V0 = 128
D0 = 256
CH = D0 + GROUP * ROW_L
QROWS = GROUP * OBS_L
PAIRS = N // 2
HALF = DOUT // 2
EXTRA = 128
FOLD = HD ** (-0.5) * 1.4426950408889634
VLIM = 20
NEG = -1e30
FAR = 1 << 30
BF = jnp.bfloat16
F32 = jnp.float32
VMEM = pl.BlockSpec(memory_space=pltpu.VMEM)
SMEM = pl.BlockSpec(memory_space=pltpu.SMEM)


def params():
    return pltpu.CompilerParams(vmem_limit_bytes=VLIM << 20)


def cost(flops, moved, exps=0):
    return pl.CostEstimate(flops=flops, bytes_accessed=moved, transcendentals=exps)


def pack_kernel(me_ref, k_hbm, v_hbm, q_hbm, d_hbm, out_ref, *rest):
    q_out, (k_ref, v_ref, q_ref, d_ref, sems) = rest[:PAIRS], rest[PAIRS:]
    loads = [
        pltpu.make_async_copy(source, target, sems.at[at])
        for at, (source, target) in enumerate(
            ((k_hbm, k_ref), (v_hbm, v_ref), (d_hbm, d_ref), (q_hbm, q_ref))
        )
    ]
    for load in loads:
        load.start()
    for at, source in ((0, k_ref), (1, v_ref)):
        loads[at].wait()
        for dest in range(N):
            head, half = dest // 2, dest % 2
            rows = slice(half * BLOCK, (half + 1) * BLOCK)
            cols = slice(head * HD, (head + 1) * HD)
            out_ref[dest, at * BLOCK : (at + 1) * BLOCK, :] = source[rows, cols]
    loads[2].wait()
    for head in range(KVH):
        pieces = []
        for h in range(GROUP):
            at = (head * GROUP + h) * HD
            pieces.append(d_ref[:, at : at + HD].astype(F32))
        block = jnp.concatenate(pieces, axis=0).astype(BF)
        out_ref[2 * head, D0:CH, :] = block
        out_ref[2 * head + 1, D0:CH, :] = block
    loads[3].wait()
    mine = me_ref[0] // 2
    for ahead in range(PAIRS):
        group = lax.rem(mine + ahead, PAIRS)
        pieces = []
        for h in range(GROUP):
            at = pl.multiple_of((group * GROUP + h) * HD, HD)
            pieces.append(q_ref[:, pl.ds(at, HD)].astype(F32))
        q_out[ahead][...] = jnp.concatenate(pieces, axis=0).astype(BF)


def pack(me, keys, values, obs, dec):
    return pl.pallas_call(
        pack_kernel,
        out_shape=[jax.ShapeDtypeStruct((N, CH, HD), BF)]
        + [jax.ShapeDtypeStruct((QROWS, HD), BF)] * PAIRS,
        in_specs=[SMEM] + [pl.BlockSpec(memory_space=pl.ANY)] * 4,
        out_specs=[VMEM] * (1 + PAIRS),
        scratch_shapes=[
            pltpu.VMEM(keys.shape, BF),
            pltpu.VMEM(values.shape, BF),
            pltpu.VMEM(obs.shape, BF),
            pltpu.VMEM(dec.shape, BF),
            pltpu.SemaphoreType.DMA((4,)),
        ],
        compiler_params=pltpu.CompilerParams(vmem_limit_bytes=60 << 20),
        cost_estimate=cost(0, 9437184, 0),
        name="pack",
    )(me, keys, values, obs, dec)


def prep_kernel(me_ref, blocks_ref, counts_ref, lens_ref, kept_ref, len_ref):
    half = lax.rem(me_ref[0], 2)
    head = me_ref[0] // 2
    lane = lax.broadcasted_iota(jnp.int32, (1, N * BLOCK), 1)
    block = 2 * (lane // BLOCK) + half
    hit = jnp.zeros((1, N * BLOCK), jnp.int32)
    count = counts_ref[head]
    for slot in range(NB):
        name = jnp.where(slot < count, blocks_ref[head, slot], -1)
        hit = jnp.where(block == name, 1, hit)
    kept_ref[...] = jnp.where(hit == 1, block * BLOCK + lane % BLOCK, FAR)
    row = lax.broadcasted_iota(jnp.int32, (GROUP * ROW_L, BLOCK), 0) & (ROW_L - 1)
    for source in range(N):
        lens = jnp.zeros((GROUP * ROW_L, BLOCK), jnp.int32)
        for r in range(ROW_L):
            lens = jnp.where(row == r, lens_ref[source * ROW_L + r], lens)
        len_ref[source * GROUP * ROW_L : (source + 1) * GROUP * ROW_L, :] = lens


def prep(me, blocks, counts, lens):
    return pl.pallas_call(
        prep_kernel,
        out_shape=(
            jax.ShapeDtypeStruct((1, N * BLOCK), jnp.int32),
            jax.ShapeDtypeStruct((N * GROUP * ROW_L, BLOCK), jnp.int32),
        ),
        in_specs=[SMEM] * 4,
        out_specs=(VMEM, VMEM),
        compiler_params=params(),
        cost_estimate=cost(0, 3145728, 0),
        name="prep",
    )(me, blocks, counts, lens)


def dot_t(a, b):
    return lax.dot_general(a, b, (((1,), (1,)), ((), ())), preferred_element_type=F32)


DROWS = 2 * HD
STATS = 16


def decode_kernel(me_ref, r_ref, kept_ref, len_ref, send_ref, keep_ref, stat_ref):
    half = lax.rem(me_ref[0], 2)
    key = r_ref[:, K0 : K0 + BLOCK, :].reshape(N * BLOCK, HD)
    val = r_ref[:, V0 : V0 + BLOCK, :].reshape(N * BLOCK, HD)
    lane = lax.broadcasted_iota(jnp.int32, (DROWS // 2, HD), 1)
    per = DROWS // (GROUP * ROW_L)
    diagonal = lane == lax.broadcasted_iota(jnp.int32, (HD, HD), 0)
    stats = []
    for chunk in range(ROWS * GROUP // DROWS):
        query = r_ref[chunk * per : (chunk + 1) * per, D0:CH, :].reshape(DROWS, HD)
        scores = dot_t(query, key)
        lens = len_ref[chunk * DROWS : (chunk + 1) * DROWS, :]
        seen = kept_ref[...] < jnp.concatenate([lens] * N, axis=1)
        scores = jnp.where(seen, scores, NEG)
        top = jnp.max(scores, axis=1, keepdims=True).astype(BF).astype(F32)
        weights = jnp.where(seen, jnp.exp2((scores - top) * FOLD), 0.0)
        total = jnp.sum(weights, axis=1, keepdims=True)
        summed = jnp.dot(weights.astype(BF), val, preferred_element_type=F32)

        def halves(x):
            x = x.reshape(per, 2, HQ * ROW_L, x.shape[1])
            low = x[:, 0].reshape(DROWS // 2, x.shape[3])
            high = x[:, 1].reshape(DROWS // 2, x.shape[3])
            mine = jnp.where(half == 0, low, high)
            other = jnp.where(half == 0, high, low)
            return mine, other

        top_mine, top_other = halves(jnp.broadcast_to(top, (DROWS, HD)))
        total_mine, total_other = halves(jnp.broadcast_to(total, (DROWS, HD)))
        sum_mine, sum_other = halves(summed)
        coarse = total_other.astype(BF).astype(F32)
        for stat in (top_other, coarse, total_other - coarse):
            stats.append(jnp.sum(jnp.where(diagonal, stat, 0.0), axis=0, keepdims=True))
        at = slice(chunk * DROWS // 2, (chunk + 1) * DROWS // 2)
        send_ref[at, :] = sum_other.astype(BF)
        keep_ref[at, :] = sum_mine
        stat_ref[at, :] = jnp.where(lane == 0, top_mine, total_mine)
    stats.append(jnp.zeros((STATS - len(stats), HD), F32))
    send_ref[ROWS * HQ :, :] = jnp.concatenate(stats, axis=0).astype(BF)


def decode(me, received, kept, lens):
    rows = ROWS * HQ
    return pl.pallas_call(
        decode_kernel,
        out_shape=(
            jax.ShapeDtypeStruct((rows + STATS, HD), BF),
            jax.ShapeDtypeStruct((rows, HD), F32),
            jax.ShapeDtypeStruct((rows, HD), F32),
        ),
        in_specs=[SMEM, VMEM, VMEM, VMEM],
        out_specs=(VMEM, VMEM, VMEM),
        compiler_params=params(),
        cost_estimate=cost(536870912, 41943040, 1048576),
        name="decode",
    )(me, received, kept, lens)


def project_kernel(me_ref, other_ref, keep_ref, stat_ref, w_ref, send_ref, own_ref):
    half = lax.rem(me_ref[0], 2)
    rows = ROWS * HQ
    other = other_ref[...].astype(F32)
    lane = lax.broadcasted_iota(jnp.int32, (HD, HD), 1)
    diagonal = lane == lax.broadcasted_iota(jnp.int32, (HD, HD), 0)

    def column(at):
        parts = []
        for chunk in range(rows // HD):
            line = other[rows + 3 * chunk + at : rows + 3 * chunk + at + 1]
            line = jnp.broadcast_to(line, (HD, HD))
            parts.append(jnp.sum(jnp.where(diagonal, line, 0.0), axis=1, keepdims=True))
        return jnp.concatenate(parts, axis=0)

    top_o = column(0)
    total_o = column(1) + column(2)
    top_m = stat_ref[:, 0:1]
    total_m = stat_ref[:, 1:2]
    top = jnp.maximum(top_o, top_m)
    fac_o = jnp.exp2((top_o - top) * FOLD)
    fac_m = jnp.exp2((top_m - top) * FOLD)
    total = total_o * fac_o + total_m * fac_m
    mixed = other[0:rows] * fac_o + keep_ref[...] * fac_m
    attended = (mixed / total).astype(BF)
    out_row = lax.broadcasted_iota(jnp.int32, (ROWS, rows), 0)
    in_row = lax.broadcasted_iota(jnp.int32, (ROWS, rows), 1)
    base = (out_row >> 2) * (HQ * ROW_L) + (out_row & 3)
    parts = []
    for h in range(HQ):
        pick = jnp.where(in_row == base + h * ROW_L, 1.0, 0.0).astype(BF)
        parts.append(jnp.dot(pick, attended, preferred_element_type=F32).astype(BF))
    flat = jnp.concatenate(parts, axis=1)
    step = 1024
    for col in range(0, HALF, step):
        at = pl.multiple_of((1 - half) * HALF + col, step)
        product = jnp.dot(flat, w_ref[:, pl.ds(at, step)], preferred_element_type=F32)
        send_ref[:, col : col + step] = product.astype(BF)
    for col in range(0, HALF, step):
        at = pl.multiple_of(half * HALF + col, step)
        product = jnp.dot(flat, w_ref[:, pl.ds(at, step)], preferred_element_type=F32)
        own_ref[:, col : col + step] = product


def project(me, other, keep, stat, w):
    return pl.pallas_call(
        project_kernel,
        out_shape=(
            jax.ShapeDtypeStruct((ROWS, HALF), BF),
            jax.ShapeDtypeStruct((ROWS, HALF), F32),
        ),
        in_specs=[SMEM] + [VMEM] * 4,
        out_specs=(VMEM, VMEM),
        compiler_params=params(),
        cost_estimate=cost(268435456, 5242880, 0),
        name="project",
    )(me, other, keep, stat, w)


def merge_kernel(own_ref, got_ref, cols_ref, out_ref):
    both = own_ref[...] + got_ref[...].astype(F32)
    for dest in range(N):
        out_ref[dest, :, 0:HALF] = both[dest * ROW_L : (dest + 1) * ROW_L, :].astype(BF)
        out_ref[dest, :, HALF:] = cols_ref[:, dest, :].astype(BF)


def merge(own, got, cols):
    return pl.pallas_call(
        merge_kernel,
        out_shape=jax.ShapeDtypeStruct((N, ROW_L, HALF + EXTRA), BF),
        in_specs=[VMEM] * 3,
        out_specs=VMEM,
        compiler_params=params(),
        cost_estimate=cost(0, 2097152, 0),
        name="merge",
    )(own, got, cols)


MERGE = 2
WROWS = MERGE * QROWS
REACH = (POOL - 1) // 2
SPAN = SEQ // 2


def score_half(me_ref, query, keys, chunk, parity, s_ref):
    half = lax.rem(me_ref[0], 2)
    mine = me_ref[0] // 2
    row = lax.broadcasted_iota(jnp.int32, (QROWS, BLOCK), 0)
    lane = lax.broadcasted_iota(jnp.int32, (QROWS, BLOCK), 1)
    diff = lane - row % OBS_L
    peak = None
    for pair in range(PAIRS):
        scores = dot_t(query, keys(pair).reshape(2 * BLOCK, HD))
        if pair == PAIRS - 1:
            shown = []
            for j in range(2):
                start = (2 * (2 * pair + j) + parity) * BLOCK
                part = []
                for k in range(MERGE):
                    ahead = chunk * MERGE + k
                    member = 1 - half if ahead == PAIRS // 2 else half
                    source = 2 * lax.rem(mine + PAIRS - ahead, PAIRS) + member
                    place = SEQ - OBS + source * OBS_L - start
                    piece = scores[k * QROWS : (k + 1) * QROWS, j * BLOCK : (j + 1) * BLOCK]
                    part.append(jnp.where(diff <= place, piece, NEG))
                shown.append(jnp.concatenate(part, axis=0))
            scores = jnp.concatenate(shown, axis=1)
        s_ref[:, pair * 2 * BLOCK : (pair + 1) * 2 * BLOCK] = scores
        best = jnp.maximum(scores[:, 0:BLOCK], scores[:, BLOCK:])
        peak = best if peak is None else jnp.maximum(peak, best)
    return jnp.max(peak, axis=1, keepdims=True) * FOLD


def first_kernel(me_ref, *refs):
    queries, (r_ref, w_ref, stat_ref, s_ref) = refs[:PAIRS], refs[PAIRS:]
    half = lax.rem(me_ref[0], 2)
    lane = lax.broadcasted_iota(jnp.int32, (WROWS, BLOCK), 1)
    for chunk in range(PAIRS // MERGE):
        query = jnp.concatenate([queries[chunk * MERGE + k][...] for k in range(MERGE)], axis=0)
        rows = slice(chunk * WROWS, (chunk + 1) * WROWS)
        top = score_half(
            me_ref,
            query,
            lambda pair: r_ref[2 * pair : 2 * pair + 2, K0 : K0 + BLOCK, :],
            chunk,
            half,
            s_ref,
        )
        total = jnp.zeros((WROWS, BLOCK), F32)
        for b in range(N):
            at = slice(b * BLOCK, (b + 1) * BLOCK)
            weight = jnp.exp2(s_ref[:, at] * FOLD - top)
            w_ref[rows, at] = weight
            total = total + weight
        total = jnp.sum(total, axis=1, keepdims=True)
        stat_ref[rows, :] = jnp.where(lane == 0, top, total)


def first_window(me, queries, received):
    rows = PAIRS * QROWS
    return pl.pallas_call(
        first_kernel,
        out_shape=(
            jax.ShapeDtypeStruct((rows, SPAN), F32),
            jax.ShapeDtypeStruct((rows, BLOCK), F32),
        ),
        in_specs=[SMEM] + [VMEM] * (PAIRS + 1),
        out_specs=(VMEM, VMEM),
        scratch_shapes=[pltpu.VMEM((WROWS, SPAN), F32)],
        compiler_params=params(),
        cost_estimate=cost(805306368, 14680064, 3145728),
        name="first",
    )(me, *queries, received)


def second_kernel(me_ref, *refs):
    queries, rest = refs[:PAIRS], refs[PAIRS:]
    x_ref, w_ref, stat_ref, out_ref, s_ref, acc_ref = rest
    half = lax.rem(me_ref[0], 2)
    acc_ref[...] = jnp.zeros_like(acc_ref)
    for chunk in range(PAIRS // MERGE):
        query = jnp.concatenate([queries[chunk * MERGE + k][...] for k in range(MERGE)], axis=0)
        rows = slice(chunk * WROWS, (chunk + 1) * WROWS)

        def keys(pair):
            return x_ref[2 * pair : 2 * pair + 2]

        far_top = score_half(me_ref, query, keys, chunk, 1 - half, s_ref)
        own_top = stat_ref[rows, 0:1]
        top = jnp.maximum(far_top, own_top)
        total = jnp.zeros((WROWS, BLOCK), F32)
        for b in range(N):
            at = slice(b * BLOCK, (b + 1) * BLOCK)
            weight = jnp.exp2(s_ref[:, at] * FOLD - top)
            s_ref[:, at] = weight
            total = total + weight
        own_fac = jnp.exp2(own_top - top)
        total = jnp.sum(total, axis=1, keepdims=True) + stat_ref[rows, 1:2] * own_fac
        far_share = 1.0 / total
        own_share = jnp.broadcast_to(own_fac * far_share, (WROWS, BLOCK))
        far_share = jnp.broadcast_to(far_share, (WROWS, BLOCK))
        for b in range(N):
            at = slice(b * BLOCK, (b + 1) * BLOCK)
            part = w_ref[rows, at] * own_share
            acc_ref[b] += jnp.sum(part.reshape(WROWS // 8, 8, BLOCK), axis=0)
            part = s_ref[:, at] * far_share
            acc_ref[N + b] += jnp.sum(part.reshape(WROWS // 8, 8, BLOCK), axis=0)
    sums = jnp.sum(acc_ref[...], axis=1)
    own, far = sums[0:N], sums[N:NB]
    low = jnp.where(half == 0, own, far)
    high = jnp.where(half == 0, far, own)
    at_row = lax.broadcasted_iota(jnp.int32, (N, BLOCK), 0)
    at_lane = lax.broadcasted_iota(jnp.int32, (N, BLOCK), 1)
    before = pltpu.roll(pltpu.roll(high, 1, 0), REACH, 1)
    after = pltpu.roll(pltpu.roll(low, N - 1, 0), REACH, 1)
    before = jnp.where((at_lane < REACH) & (at_row > 0), before, 0.0)
    after_here = (at_lane >= REACH) & (at_lane < 2 * REACH) & (at_row < N - 1)
    out_ref[0] = low
    out_ref[1] = high
    out_ref[2] = jnp.where(after_here, after, before)
    out_ref[3] = jnp.zeros_like(low)


def second_window(me, queries, partner, weights, stat):
    return pl.pallas_call(
        second_kernel,
        out_shape=jax.ShapeDtypeStruct((ROW_L, N, BLOCK), F32),
        in_specs=[SMEM] + [VMEM] * (PAIRS + 3),
        out_specs=VMEM,
        scratch_shapes=[
            pltpu.VMEM((WROWS, SPAN), F32),
            pltpu.VMEM((NB, 8, BLOCK), F32),
        ],
        compiler_params=params(),
        cost_estimate=cost(805306368, 25165824, 3145728),
        name="second",
    )(me, *queries, partner, weights, stat)


def finish_kernel(back_ref, pooled_ref, out_ref):
    step = 512
    for part in range(2):
        for col in range(0, HALF, step):
            total = back_ref[part, :, col : col + step].astype(F32)
            for pair in range(1, PAIRS):
                total = total + back_ref[2 * pair + part, :, col : col + step].astype(F32)
            out_ref[:, part * HALF + col : part * HALF + col + step] = total.astype(BF)
    lows, highs, edges = [], [], []
    for head in range(KVH):
        cols = back_ref[2 * head, :, HALF:].astype(F32) + back_ref[2 * head + 1, :, HALF:].astype(F32)
        lows.append(cols[0:1])
        highs.append(cols[1:2])
        edges.append(cols[2:3])
    body = jnp.concatenate(
        [jnp.concatenate(lows, axis=0), jnp.concatenate(highs, axis=0)], axis=1
    )
    edge = jnp.concatenate(edges, axis=0)
    width = 2 * BLOCK
    edge = jnp.concatenate([edge, jnp.zeros_like(edge)], axis=1)
    lane = lax.broadcasted_iota(jnp.int32, (KVH, width), 1)
    pooled = None
    for offset in range(-REACH, REACH + 1):
        if offset < 0:
            moved = pltpu.roll(body, -offset, 1)
            rest = pltpu.roll(edge, (width - (REACH + offset)) % width, 1)
            term = jnp.where(lane < -offset, rest, moved)
        elif offset > 0:
            moved = pltpu.roll(body, width - offset, 1)
            rest = pltpu.roll(edge, width - offset - REACH, 1)
            term = jnp.where(lane >= width - offset, rest, moved)
        else:
            term = body
        pooled = term if pooled is None else pooled + term
    pooled_ref[...] = pooled / POOL


def finish(back):
    return pl.pallas_call(
        finish_kernel,
        out_shape=(
            jax.ShapeDtypeStruct((KVH, 2 * BLOCK), F32),
            jax.ShapeDtypeStruct((ROW_L, DOUT), BF),
        ),
        in_specs=[VMEM],
        out_specs=(VMEM, VMEM),
        compiler_params=params(),
        cost_estimate=cost(0, 2097152, 0),
        name="finish",
    )(back)


def shards(keys, values, obs_queries, dec_queries, kept_blocks, kept_counts, dec_lengths, out_proj):
    swap = [(i, i ^ 1) for i in range(N)]
    side = [(i, (i + 1 if i % 2 else i - 1) % N) for i in range(N)]
    me = lax.axis_index("ctx")[None].astype(jnp.int32)
    sent, *ask = pack(me, keys, values, obs_queries, dec_queries.reshape(ROW_L, H * HD))
    received = lax.all_to_all(sent, "ctx", 0, 0, tiled=True)
    queries = [ask[0]]
    for ahead in range(1, PAIRS):
        ring = [
            (i, (i + 2 * ahead + (0 if 2 * ahead != PAIRS else 1 - 2 * (i % 2))) % N)
            for i in range(N)
        ]
        queries.append(lax.ppermute(ask[ahead], "ctx", ring))
    kept, lens = prep(me, kept_blocks, kept_counts, dec_lengths)
    partner = lax.ppermute(received[:, K0 : K0 + BLOCK, :], "ctx", swap)
    send, keep, stat = decode(me, received, kept, lens)
    other = lax.ppermute(send, "ctx", swap)
    part, part_stat = first_window(me, queries, received)
    give, own = project(me, other, keep, stat, out_proj)
    got = lax.ppermute(give, "ctx", side)
    cols = second_window(me, queries, partner, part, part_stat)
    both = merge(own, got, cols)
    back = lax.all_to_all(both, "ctx", 0, 0, tiled=True)
    pooled, decoded = finish(back)
    return pooled, decoded[:, None, :]


def solution(mesh):
    return jax.shard_map(
        shards,
        mesh=mesh,
        in_specs=(
            P(("req", "ctx"), None),
            P(("req", "ctx"), None),
            P(("req", "ctx"), None),
            P(("req", "ctx"), None, None),
            P("req", None),
            P("req"),
            P("req"),
            P("ctx", None),
        ),
        out_specs=(P(None, ("req", "ctx")), P(("req", "ctx"), None, None)),
        check_vma=False,
    )
```
